512 devices in a mesh: blk: 16 (over y_hi, x, core), wide: 32 (over y_lo, z).
Axes of the slice: x: 4, y: 4 (y_hi: 2, y_lo: 2; y = y_hi * 2 + y_lo), z: 16, core: 2. Of those that a mesh axis runs over, the one named last changes fastest.
Arguments:
- patch_keys: float32 [512, 196, 512], P(('blk', 'wide')), may hold values from -16 to 16
- patch_values: float32 [512, 196, 512], P(('blk', 'wide')), may hold values from -6 to 6
- caption_queries: float32 [512, 512], P(('blk', 'wide')), may hold values from -48 to 48
- positive: int32 [512, 512], P(('blk', 'wide')), may hold values 0 or 1
Outputs:
- grad_keys: float32 [512, 196, 512], P(('blk', 'wide'))
- grad_values: float32 [512, 196, 512], P(('blk', 'wide'))
- grad_queries: float32 [512, 512], P(('blk', 'wide'))
The draws below stay inside these ranges and needn't reach their ends.
All inputs are finite; a program needn't handle non-finite values. No bound on the sum of `positive` on one device may be relied on, other than what follows from the above.
Results may differ from the reference program's by a relative error of at most 0.0005.
Values sent between devices are 32-bit elements; how exact they have to be, the bound alone decides.
No kernel may reach another device: no remote copies, remote signals or barrier semaphores. Data moves between devices by JAX's collectives and lax.ppermute only.
A program may use at most 64 MiB of HBM per device.

```python
import jax
import jax.numpy as jnp
from jax import lax

D = 512
HEADS = 8
PATCHES = 196
IMAGES = 512
CAPTIONS = 512


def draw_patch_keys(key, part):
    shape = (IMAGES, PATCHES, D)
    base = jax.random.truncated_normal(jax.random.fold_in(key, 11), -5.0, 5.0, shape, jnp.float32)
    return base


def draw_caption_queries(key, part):
    shape = (CAPTIONS, D)
    scales = jnp.exp(jax.random.uniform(jax.random.fold_in(key, 13), (CAPTIONS, 1), jnp.float32, jnp.log(0.3), jnp.log(3.0)))
    base = jax.random.truncated_normal(jax.random.fold_in(key, 17), -5.0, 5.0, shape, jnp.float32) * scales
    return base


def plant(entries, own_key, least, largest):
    spot = [jax.random.randint(jax.random.fold_in(own_key, axis), (), 0, length) for axis, length in enumerate(entries.shape)]
    widest = entries.shape.index(max(entries.shape))
    neighbour = spot[:widest] + [(spot[widest] + 1) % entries.shape[widest]] + spot[widest + 1:]
    return entries.at[tuple(spot)].set(least).at[tuple(neighbour)].set(largest)


def level_of(stream_key, extent, split, smallest, high):
    def one(axis_at, blocks):
        heights = jax.random.uniform(jax.random.fold_in(jax.random.fold_in(stream_key, 6), axis_at), (blocks,), jnp.float32, smallest / len(split), high / len(split))
        return jnp.repeat(jnp.exp(heights), extent[axis_at] // blocks).reshape((-1,) + (1,) * (len(extent) - axis_at - 1))

    level = one(*split[0])
    for cut in split[1:]:
        level = level * one(*cut)
    return level


def noise(own_key, extent, scale, bound, cuts=(), dtype=jnp.bfloat16):
    values = jax.random.normal(own_key, extent, jnp.float32) * scale
    if len(cuts) > 0:
        values = level_of(own_key, extent, cuts, -0.22, 0.18) * values
    return jnp.clip(values, min=-bound, max=bound).astype(dtype)


def setup_inputs(seed: int = 0) -> dict:
    key_of = jax.random.split(jax.random.key(seed), 5)
    patch_keys = draw_patch_keys(jax.random.fold_in(key_of[4], 71), 0)
    patch_values = noise(key_of[1], (IMAGES, PATCHES, D), 1.0, 6.0, ((0, 512),), jnp.float32)
    caption_queries = draw_caption_queries(jax.random.fold_in(key_of[4], 71), 0)
    positive = plant((jax.random.randint(key_of[3], (IMAGES, CAPTIONS), 0, 128) < 1).astype(jnp.int32), jax.random.fold_in(key_of[3], 1), 0, 1)
    return dict(patch_keys=patch_keys, patch_values=patch_values, caption_queries=caption_queries, positive=positive)


epsilon = 1e-06
similarity_multiplier = 10.0
similarity_shift_term = -2.0

def pair_loss(keys, values, queries, labels):
    images, patches, width = keys.shape
    row_count = queries.shape[0]
    head_dim = width // HEADS
    query_heads = queries.reshape(row_count, HEADS, head_dim)
    key_heads = keys.reshape(images, patches, HEADS, head_dim)
    value_heads = values.reshape(images, patches, HEADS, head_dim)
    scores = jnp.einsum('chd,iphd->ichp', query_heads, key_heads, precision=lax.Precision.HIGHEST) * head_dim ** (-0.5)
    row_max = lax.stop_gradient(lax.optimization_barrier(jnp.max(scores, axis=3, keepdims=True)))
    exponent = jnp.exp(scores - row_max)
    weights = exponent / lax.optimization_barrier(jnp.sum(exponent, axis=3, keepdims=True))
    pooled = jnp.einsum('ichp,iphd->ichd', weights, value_heads, precision=lax.Precision.HIGHEST).reshape(images, row_count, width)
    matching_similarity = lax.optimization_barrier(jnp.mean(pooled * queries[None], axis=2))
    summary_reciprocal_length = lax.rsqrt(lax.optimization_barrier(jnp.mean(pooled * pooled, axis=2)) + epsilon)
    probe_reciprocal_length = lax.rsqrt(lax.optimization_barrier(jnp.mean(queries * queries, axis=1)) + epsilon)
    matching_scaled_scores = similarity_multiplier * matching_similarity * summary_reciprocal_length * probe_reciprocal_length[None] + similarity_shift_term
    label_signs = 2.0 * labels.astype(jnp.float32) - 1.0
    return jnp.sum(jnp.logaddexp(0.0, -label_signs * matching_scaled_scores))

def reference(patch_keys, patch_values, caption_queries, positive):

    def image_step(query_total, packed):
        one_keys, one_values, one_labels = packed

        def loss_of(keys_in, values_in, input_queries):
            return pair_loss(keys_in[None], values_in[None], input_queries, one_labels[None])
        total, pull_back = jax.vjp(loss_of, one_keys, one_values, caption_queries)
        key_part, value_part, query_part = pull_back(jnp.ones_like(total))
        return (query_total + query_part, (key_part, value_part))
    query_total, (grad_keys, grad_values) = lax.scan(image_step, jnp.zeros_like(caption_queries), (patch_keys, patch_values, positive))
    return (grad_keys, grad_values, query_total)
```

```python
import functools
import math

import jax
import jax.numpy as jnp
from jax import lax
from jax.experimental import pallas as pl
from jax.experimental.pallas import tpu as pltpu
from jax.sharding import Mesh
from jax.sharding import PartitionSpec as P

HEADS = 8
HEAD_DIM = 64
ROWS = 208
LOG2E = math.log2(math.e)
LN2 = math.log(2.0)


def split(x):
    high = x.astype(jnp.bfloat16)
    return high, (x - high.astype(jnp.float32)).astype(jnp.bfloat16)


def product(lhs, rhs, transposed=False):
    contract = ((1,), (1 if transposed else 0,))
    return lax.dot_general(lhs, rhs, (contract, ((), ())), preferred_element_type=jnp.float32)


def prepare_kernel(k_ref, v_ref, kc_ref, vc_ref, kt_ref, vt_ref, pad_ref):
    patches = k_ref.shape[0]
    for source, cat_ref, turned_ref in ((k_ref, kc_ref, kt_ref), (v_ref, vc_ref, vt_ref)):
        pad_ref[192:, :] = jnp.zeros((64, 512), jnp.float32)
        pad_ref[:patches, :] = source[...]
        left = lax.broadcasted_iota(jnp.int32, (ROWS, 128), 1) < HEAD_DIM
        for pair in range(HEADS // 2):
            tile = pad_ref[:, pair * 128:(pair + 1) * 128]
            rows = tile[:ROWS]
            high = rows.astype(jnp.bfloat16).astype(jnp.float32)
            for place, part in ((0, high), (1, rows - high)):
                rolled = pltpu.roll(part, HEAD_DIM, 1)
                lanes = slice(place * 128, (place + 1) * 128)
                cat_ref[2 * pair, :, lanes] = jnp.where(left, part, rolled).astype(jnp.bfloat16)
                cat_ref[2 * pair + 1, :, lanes] = jnp.where(left, rolled, part).astype(jnp.bfloat16)
            turned_high, turned_low = split(tile.T)
            for side in range(2):
                own = slice(side * HEAD_DIM, (side + 1) * HEAD_DIM)
                turned_ref[2 * pair + side, :HEAD_DIM, :] = turned_high[own, :ROWS]
                turned_ref[2 * pair + side, HEAD_DIM:, :] = turned_low[own, :ROWS]


def prepare(k, v):
    cat = jax.ShapeDtypeStruct((HEADS, ROWS, 256), jnp.bfloat16)
    turned = jax.ShapeDtypeStruct((HEADS, 128, ROWS), jnp.bfloat16)
    return pl.pallas_call(
        prepare_kernel,
        out_shape=(cat, cat, turned, turned),
        scratch_shapes=[pltpu.VMEM((256, 512), jnp.float32)],
        name="prepare",
    )(k, v)


def chunk_grads(q, label, kc_ref, vc_ref, kt_ref, vt_ref, key_acc, value_acc, e_ref, eh_ref, el_ref, o_ref, first):
    columns = q.shape[0]
    turned = q.T
    query_high, query_low = split(turned * (LOG2E / 8.0))
    inverse = []
    match = jnp.zeros((1, columns), jnp.float32)
    square = jnp.zeros((1, columns), jnp.float32)
    below = lax.broadcasted_iota(jnp.int32, (16, columns), 0) < 4
    for head in range(HEADS):
        own = slice(head * HEAD_DIM, (head + 1) * HEAD_DIM)
        qh, ql = query_high[own], query_low[own]
        scores = product(kc_ref[head], jnp.concatenate([qh, ql, qh, ql], 0))
        scores = jnp.concatenate([scores[:192], jnp.where(below, scores[192:], -1e30)], 0)
        exponent = jnp.exp2(scores - jnp.max(scores, axis=0, keepdims=True))
        inverse.append(1.0 / jnp.sum(exponent, axis=0, keepdims=True))
        high, low = split(exponent)
        e_ref[head] = exponent
        eh_ref[head] = high
        el_ref[head] = low
        wide = product(vt_ref[head], high)
        pooled = (wide[:HEAD_DIM] + wide[HEAD_DIM:] + product(vt_ref[head, :HEAD_DIM], low)) * inverse[head]
        o_ref[own, :] = pooled
        match += jnp.sum(pooled * turned[own], axis=0, keepdims=True)
        square += jnp.sum(pooled * pooled, axis=0, keepdims=True)
    width = HEADS * HEAD_DIM
    match = match / width
    summary = lax.rsqrt(square / width + 1e-6)
    probe = lax.rsqrt(jnp.sum(turned * turned, axis=0, keepdims=True) / width + 1e-6)
    sign = 2.0 * label.astype(jnp.float32) - 1.0
    logit = 10.0 * match * summary * probe - 2.0
    slope = -sign / (1.0 + jnp.exp(sign * logit)) * (10.0 / width)
    alpha = slope * summary * probe
    beta = -alpha * match * summary * summary
    gamma = -alpha * match * probe * probe
    parts = []
    for head in range(HEADS):
        own = slice(head * HEAD_DIM, (head + 1) * HEAD_DIM)
        pooled = o_ref[own, :]
        query = turned[own]
        grad = (alpha * query + beta * pooled) * inverse[head]
        delta = jnp.sum(grad * pooled, axis=0, keepdims=True)
        gh, gl = split(grad)
        inner = product(vc_ref[head], jnp.concatenate([gh, gl, gh, gl], 0))
        score_high, score_low = split(e_ref[head] * (inner - delta))
        both = jnp.concatenate([gh, gl], 0)
        value_part = product(eh_ref[head], both, True) + product(el_ref[head], both, True)
        both = jnp.concatenate([query_high[own], query_low[own]], 0)
        key_part = product(score_high, both, True) + product(score_low, both, True)
        if first:
            value_acc[head] = value_part
            key_acc[head] = key_part
        else:
            value_acc[head] += value_part
            key_acc[head] += key_part
        wide = product(kt_ref[head], score_high)
        through = wide[:HEAD_DIM] + wide[HEAD_DIM:] + product(kt_ref[head, :HEAD_DIM], score_low)
        parts.append(through * 0.125 + alpha * pooled + gamma * query)
    return jnp.concatenate(parts, 0).T


def folded(acc, out_ref, scale):
    patches = out_ref.shape[0]
    left = lax.broadcasted_iota(jnp.int32, (ROWS, 128), 1) < HEAD_DIM
    for pair in range(HEADS // 2):
        even, odd = acc[2 * pair], acc[2 * pair + 1]
        whole = jnp.where(left, even + pltpu.roll(even, HEAD_DIM, 1), odd + pltpu.roll(odd, HEAD_DIM, 1))
        out_ref[:, pair * 128:(pair + 1) * 128] = (whole * scale)[:patches]


def grads_kernel(first, last, chunk, *refs):
    q_ref, label_ref, kc_ref, vc_ref, kt_ref, vt_ref = refs[:6]
    refs = refs[6:]
    if not first:
        key_in, value_in = refs[:2]
        refs = refs[2:]
    dq_ref, dk_ref, dv_ref = refs[:3]
    if last:
        key_acc, value_acc = refs[3:5]
        scratch = refs[5:]
    else:
        key_acc, value_acc = dk_ref, dv_ref
        scratch = refs[3:]
    if not first:
        key_acc[...] = key_in[...]
        value_acc[...] = value_in[...]
    for start in range(0, q_ref.shape[0], chunk):
        part = slice(start, start + chunk)
        dq_ref[part, :] = chunk_grads(
            q_ref[part, :], label_ref[:, part], kc_ref, vc_ref, kt_ref, vt_ref,
            key_acc, value_acc, *scratch, first and start == 0)
    if last:
        folded(key_acc, dk_ref, LN2)
        folded(value_acc, dv_ref, 1.0)


def grads(q, label, prepared, acc=(), last=True, patches=196):
    rows = q.shape[0]
    chunk = min(rows, 256)
    acc_shape = (HEADS, ROWS, 128)
    big = jax.ShapeDtypeStruct((patches, 512) if last else acc_shape, jnp.float32)
    own_acc = [pltpu.VMEM(acc_shape, jnp.float32)] * 2 if last else []
    return pl.pallas_call(
        functools.partial(grads_kernel, not acc, last, chunk),
        out_shape=(jax.ShapeDtypeStruct((rows, 512), jnp.float32), big, big),
        scratch_shapes=own_acc + [
            pltpu.VMEM((HEADS, ROWS, chunk), jnp.float32),
            pltpu.VMEM((HEADS, ROWS, chunk), jnp.bfloat16),
            pltpu.VMEM((HEADS, ROWS, chunk), jnp.bfloat16),
            pltpu.VMEM((512, chunk), jnp.float32),
        ],
        name="grads",
    )(q, label, *prepared, *acc)


RING = ("y_hi", "x", "y_lo")


def spread(value, axis, count):
    return lax.all_to_all(jnp.broadcast_to(value[None], (count,) + value.shape), axis, 0, 0, tiled=True)


def swapped(value):
    return lax.ppermute(value, "core", [(0, 1), (1, 0)])


def per_device(patch_keys, patch_values, caption_queries, positive):
    sides = positive.reshape(8, 2, 32).swapaxes(0, 1).reshape(2, 1, 256)
    core = lax.axis_index("core")
    own_label = lax.dynamic_index_in_dim(sides, core, 0, keepdims=False)
    other_label = lax.dynamic_index_in_dim(sides, 1 - core, 0, keepdims=False)
    prepared = prepare(patch_keys[0], patch_values[0])
    row = spread(caption_queries, "z", 16).reshape(16, 512)
    own = spread(row, RING, 16).reshape(256, 512)
    other = swapped(own)
    dq_first, *acc = grads(own[:128], own_label[:, :128], prepared, last=False)
    dq_other, *acc = grads(other, other_label, prepared, acc, last=False)
    received = swapped(dq_other)
    dq_second, grad_keys, grad_values = grads(own[128:], own_label[:, 128:], prepared, acc)
    total = jnp.concatenate([dq_first, dq_second], 0) + received
    total = lax.all_to_all(total.reshape(16, 16, 512), RING, 0, 0, tiled=True).sum(0)
    total = lax.all_to_all(total.reshape(16, 1, 512), "z", 0, 0, tiled=True).sum(0)
    return grad_keys[None], grad_values[None], total


AXES = ("y_hi", "x", "core", "y_lo", "z")


def solution(mesh):
    fine = Mesh(mesh.devices.reshape(2, 4, 2, 2, 16), AXES)
    return jax.shard_map(
        per_device, mesh=fine,
        in_specs=(P(AXES, None, None), P(AXES, None, None), P(AXES, None), P(AXES, None)),
        out_specs=(P(AXES, None, None), P(AXES, None, None), P(AXES, None)),
        check_vma=False,
    )
```

```python
import math

import jax
import jax.numpy as jnp
from jax import lax
from jax.experimental import pallas as pl
from jax.experimental.pallas import tpu as pltpu
from jax.sharding import Mesh
from jax.sharding import PartitionSpec as P


HEADS = 8
HEAD_DIM = 64
PATCHES = 196
ROWS = 208
PART = 208
LOG2E = math.log2(math.e)
LN2 = math.log(2.0)
PARAMS = pltpu.CompilerParams(vmem_limit_bytes=24 * 1024 * 1024)


def split(x):
    high = x.astype(jnp.bfloat16)
    return high, (x - high.astype(jnp.float32)).astype(jnp.bfloat16)


def product(lhs, rhs, transposed=False):
    contract = ((1,), (1 if transposed else 0,))
    return lax.dot_general(lhs, rhs, (contract, ((), ())), preferred_element_type=jnp.float32)


def pack_kernel(k_ref, v_ref, label_ref, out_ref):
    out_ref[:PATCHES, :] = k_ref[:, 0, :]
    out_ref[PART:PART + PATCHES, :] = v_ref[:, 0, :]
    labels = jnp.broadcast_to(label_ref[...].astype(jnp.float32), (8, 512))
    out_ref[2 * PART - 8:, :] = labels


def pack(k, v, label):
    return pl.pallas_call(
        pack_kernel,
        out_shape=pltpu.VMEM((2 * PART, 512), jnp.float32),
        name="pack",
        compiler_params=PARAMS,
    )(k, v, label)


def prepare_kernel(packed_ref, kc_ref, vc_ref, kt_ref, vt_ref, label_ref, pad_ref):
    for start, cat_ref, turned_ref in ((0, kc_ref, kt_ref), (PART, vc_ref, vt_ref)):
        pad_ref[192:, :] = jnp.zeros((64, 512), jnp.float32)
        pad_ref[:PATCHES, :] = packed_ref[start:start + PATCHES, :]
        left = lax.broadcasted_iota(jnp.int32, (ROWS, 128), 1) < HEAD_DIM
        for pair in range(HEADS // 2):
            tile = pad_ref[:, pair * 128:(pair + 1) * 128]
            rows = tile[:ROWS]
            high = rows.astype(jnp.bfloat16).astype(jnp.float32)
            for place, part in ((0, high), (1, rows - high)):
                rolled = pltpu.roll(part, HEAD_DIM, 1)
                lanes = slice(place * 128, (place + 1) * 128)
                cat_ref[2 * pair, :, lanes] = jnp.where(left, part, rolled).astype(jnp.bfloat16)
                cat_ref[2 * pair + 1, :, lanes] = jnp.where(left, rolled, part).astype(jnp.bfloat16)
            turned_high, turned_low = split(tile.T)
            for side in range(2):
                own = slice(side * HEAD_DIM, (side + 1) * HEAD_DIM)
                turned_ref[2 * pair + side, :HEAD_DIM, :] = turned_high[own, :ROWS]
                turned_ref[2 * pair + side, HEAD_DIM:, :] = turned_low[own, :ROWS]
    label_ref[...] = packed_ref[2 * PART - 8:, :]


def prepare(packed):
    cat = pltpu.VMEM((HEADS, ROWS, 256), jnp.bfloat16)
    turned = pltpu.VMEM((HEADS, 128, ROWS), jnp.bfloat16)
    return pl.pallas_call(
        prepare_kernel,
        out_shape=(cat, cat, turned, turned, pltpu.VMEM((8, 512), jnp.float32)),
        scratch_shapes=[pltpu.VMEM((256, 512), jnp.float32)],
        name="prepare",
        compiler_params=PARAMS,
    )(*in_vmem(packed))


def folded(even, odd, scale, out_ref, start, lanes):
    left = lax.broadcasted_iota(jnp.int32, (ROWS, 128), 1) < HEAD_DIM
    whole = jnp.where(left, even + pltpu.roll(even, HEAD_DIM, 1), odd + pltpu.roll(odd, HEAD_DIM, 1))
    out_ref[start:start + ROWS, lanes] = whole * scale


def image_grads(turned, query_high, query_low, label, kc_ref, vc_ref, kt_ref, vt_ref, image_ref,
                e_ref, eh_ref, el_ref, o_ref):
    columns = turned.shape[1]
    inverse = []
    match = jnp.zeros((1, columns), jnp.float32)
    square = jnp.zeros((1, columns), jnp.float32)
    below = lax.broadcasted_iota(jnp.int32, (16, columns), 0) < 4
    for head in range(HEADS):
        own = slice(head * HEAD_DIM, (head + 1) * HEAD_DIM)
        qh, ql = query_high[own], query_low[own]
        scores = product(kc_ref[head], jnp.concatenate([qh, ql, qh, ql], 0))
        scores = jnp.concatenate([scores[:192], jnp.where(below, scores[192:], -1e30)], 0)
        exponent = jnp.exp2(scores - jnp.max(scores, axis=0, keepdims=True))
        inverse.append(1.0 / jnp.sum(exponent, axis=0, keepdims=True))
        high, low = split(exponent)
        e_ref[head] = exponent
        eh_ref[head] = high
        el_ref[head] = low
        wide = product(vt_ref[head], high)
        pooled = (wide[:HEAD_DIM] + wide[HEAD_DIM:] + product(vt_ref[head, :HEAD_DIM], low)) * inverse[head]
        o_ref[own, :] = pooled
        match += jnp.sum(pooled * turned[own], axis=0, keepdims=True)
        square += jnp.sum(pooled * pooled, axis=0, keepdims=True)
    width = HEADS * HEAD_DIM
    match = match / width
    summary = lax.rsqrt(square / width + 1e-6)
    probe = lax.rsqrt(jnp.sum(turned * turned, axis=0, keepdims=True) / width + 1e-6)
    sign = 2.0 * label - 1.0
    logit = 10.0 * match * summary * probe - 2.0
    slope = -sign / (1.0 + jnp.exp(sign * logit)) * (10.0 / width)
    alpha = slope * summary * probe
    beta = -alpha * match * summary * summary
    gamma = -alpha * match * probe * probe
    parts = []
    for head in range(HEADS):
        own = slice(head * HEAD_DIM, (head + 1) * HEAD_DIM)
        pooled = o_ref[own, :]
        query = turned[own]
        grad = (alpha * query + beta * pooled) * inverse[head]
        delta = jnp.sum(grad * pooled, axis=0, keepdims=True)
        gh, gl = split(grad)
        inner = product(vc_ref[head], jnp.concatenate([gh, gl, gh, gl], 0))
        score_high, score_low = split(e_ref[head] * (inner - delta))
        both = jnp.concatenate([gh, gl], 0)
        value_part = product(eh_ref[head], both, True) + product(el_ref[head], both, True)
        both = jnp.concatenate([query_high[own], query_low[own]], 0)
        key_part = product(score_high, both, True) + product(score_low, both, True)
        if head % 2 == 0:
            even = key_part, value_part
        else:
            lanes = slice((head - 1) * HEAD_DIM, (head + 1) * HEAD_DIM)
            folded(even[0], key_part, LN2, image_ref, 0, lanes)
            folded(even[1], value_part, 1.0, image_ref, PART, lanes)
        wide = product(kt_ref[head], score_high)
        through = wide[:HEAD_DIM] + wide[HEAD_DIM:] + product(kt_ref[head, :HEAD_DIM], score_low)
        parts.append(through * 0.125 + alpha * pooled + gamma * query)
    return jnp.concatenate(parts, 0)


def columns_of(label_ref, core):
    blocks = [label_ref[:1, start:start + 32] for start in range(0, 512, 32)]
    sides = [jnp.concatenate(blocks[side::2], 1) for side in range(2)]
    return jnp.where(core == 0, sides[0], sides[1])


def grads_kernel(core_ref, q_ref, *refs):
    images = (refs[:5], refs[5:10])
    dq_ref, *totals = refs[10:13]
    scratch = refs[13:]
    turned = q_ref[...].T
    query_high, query_low = split(turned * (LOG2E / 8.0))
    grad = 0.0
    for image in range(2):
        *arrays, label_ref = images[image]
        label = columns_of(label_ref, core_ref[0])
        grad += image_grads(turned, query_high, query_low, label, *arrays, totals[image], *scratch)
    dq_ref[...] = grad.T


def in_vmem(*values):
    return [pltpu.with_memory_space_constraint(value, pltpu.VMEM) for value in values]


def grads(core, q, own, other):
    chunk = q.shape[0]
    total = pltpu.VMEM((2 * PART, 512), jnp.float32)
    return pl.pallas_call(
        grads_kernel,
        in_specs=[pl.BlockSpec(memory_space=pltpu.SMEM)] + [pl.BlockSpec(memory_space=pltpu.VMEM)] * 11,
        out_shape=(pltpu.VMEM((chunk, 512), jnp.float32), total, total),
        scratch_shapes=[
            pltpu.VMEM((HEADS, ROWS, chunk), jnp.float32),
            pltpu.VMEM((HEADS, ROWS, chunk), jnp.bfloat16),
            pltpu.VMEM((HEADS, ROWS, chunk), jnp.bfloat16),
            pltpu.VMEM((512, chunk), jnp.float32),
        ],
        name="grads",
        compiler_params=PARAMS,
    )(core, *in_vmem(q, *own, *other))


def finish_kernel(own_ref, received_ref, dk_ref, dv_ref):
    for start, out_ref in ((0, dk_ref), (PART, dv_ref)):
        rows = slice(start, start + PATCHES)
        out_ref[:, 0, :] = own_ref[rows, :] + received_ref[rows, :]


def finish(own, received):
    out = jax.ShapeDtypeStruct((PATCHES, 1, 512), jnp.float32)
    return pl.pallas_call(
        finish_kernel, out_shape=(out, out), name="finish", compiler_params=PARAMS,
    )(*in_vmem(own, received))


RING = ("y_hi", "x", "y_lo")


def spread(value, axis, count):
    return lax.all_to_all(jnp.broadcast_to(value[None], (count,) + value.shape), axis, 0, 0, tiled=True)


def swapped(value):
    return lax.ppermute(value, "core", [(0, 1), (1, 0)])


def per_device(patch_keys, patch_values, caption_queries, positive):
    core = lax.axis_index("core").astype(jnp.int32).reshape(1)
    packed = pack(patch_keys.swapaxes(0, 1), patch_values.swapaxes(0, 1), positive)
    row = spread(caption_queries, "z", 16).reshape(16, 512)
    row, packed = lax.optimization_barrier((row, packed))
    queries = spread(row, RING, 16).reshape(256, 512)
    other = swapped(packed)
    queries, packed, other = lax.optimization_barrier((queries, packed, other))
    dq, own, foreign = grads(core, queries, prepare(packed), prepare(other))
    total = lax.all_to_all(dq.reshape(16, 16, 512), RING, 0, 0, tiled=True).sum(0)
    received = swapped(foreign)
    total = lax.all_to_all(total.reshape(16, 1, 512), "z", 0, 0, tiled=True).sum(0)
    grad_keys, grad_values = finish(own, received)
    return grad_keys.swapaxes(0, 1), grad_values.swapaxes(0, 1), total


AXES = ("y_hi", "x", "core", "y_lo", "z")


def solution(mesh):
    fine = Mesh(mesh.devices.reshape(2, 4, 2, 2, 16), AXES)
    return jax.shard_map(
        per_device, mesh=fine,
        in_specs=(P(AXES, None, None), P(AXES, None, None), P(AXES, None), P(AXES, None)),
        out_specs=(P(AXES, None, None), P(AXES, None, None), P(AXES, None)),
        check_vma=False,
    )
```

```python
import math

import jax
import jax.numpy as jnp
from jax import lax
from jax.experimental import pallas as pl
from jax.experimental.pallas import tpu as pltpu
from jax.sharding import Mesh
from jax.sharding import PartitionSpec as P


HEADS = 8
HEAD_DIM = 64
PATCHES = 196
ROWS = 208
PART = 208
LOG2E = math.log2(math.e)
LN2 = math.log(2.0)
PARAMS = pltpu.CompilerParams(vmem_limit_bytes=24 * 1024 * 1024)


def split(x):
    high = x.astype(jnp.bfloat16)
    return high, (x - high.astype(jnp.float32)).astype(jnp.bfloat16)


def product(lhs, rhs, transposed=False):
    contract = ((1,), (1 if transposed else 0,))
    return lax.dot_general(lhs, rhs, (contract, ((), ())), preferred_element_type=jnp.float32)


def pack_kernel(k_ref, v_ref, label_ref, out_ref):
    out_ref[:PATCHES, :] = k_ref[:, 0, :]
    out_ref[PART:PART + PATCHES, :] = v_ref[:, 0, :]
    labels = jnp.broadcast_to(label_ref[...].astype(jnp.float32), (8, 512))
    out_ref[2 * PART - 8:, :] = labels


def pack(k, v, label):
    return pl.pallas_call(
        pack_kernel,
        out_shape=pltpu.VMEM((2 * PART, 512), jnp.float32),
        name="pack",
        compiler_params=PARAMS,
    )(k, v, label)


def prepare_kernel(packed_ref, kc_ref, vc_ref, kt_ref, vt_ref, label_ref, pad_ref):
    for start, cat_ref, turned_ref, scale in ((0, kc_ref, kt_ref, 0.125), (PART, vc_ref, vt_ref, 1.0)):
        pad_ref[192:, :] = jnp.zeros((64, 512), jnp.float32)
        pad_ref[:PATCHES, :] = packed_ref[start:start + PATCHES, :]
        left = lax.broadcasted_iota(jnp.int32, (ROWS, 128), 1) < HEAD_DIM
        for pair in range(HEADS // 2):
            tile = pad_ref[:, pair * 128:(pair + 1) * 128]
            rows = tile[:ROWS]
            high = rows.astype(jnp.bfloat16).astype(jnp.float32)
            for place, part in ((0, high), (1, rows - high)):
                rolled = pltpu.roll(part, HEAD_DIM, 1)
                lanes = slice(place * 128, (place + 1) * 128)
                cat_ref[2 * pair, :, lanes] = jnp.where(left, part, rolled).astype(jnp.bfloat16)
                cat_ref[2 * pair + 1, :, lanes] = jnp.where(left, rolled, part).astype(jnp.bfloat16)
            turned_high, turned_low = split(tile.T * scale)
            for side in range(2):
                own = slice(side * HEAD_DIM, (side + 1) * HEAD_DIM)
                turned_ref[2 * pair + side, :HEAD_DIM, :] = turned_high[own, :ROWS]
                turned_ref[2 * pair + side, HEAD_DIM:, :] = turned_low[own, :ROWS]
    label_ref[...] = packed_ref[2 * PART - 8:, :]


def prepare(packed):
    cat = pltpu.VMEM((HEADS, ROWS, 256), jnp.bfloat16)
    turned = pltpu.VMEM((HEADS, 128, ROWS), jnp.bfloat16)
    return pl.pallas_call(
        prepare_kernel,
        out_shape=(cat, cat, turned, turned, pltpu.VMEM((8, 512), jnp.float32)),
        scratch_shapes=[pltpu.VMEM((256, 512), jnp.float32)],
        name="prepare",
        compiler_params=PARAMS,
    )(*in_vmem(packed))


def folded(even, odd):
    left = lax.broadcasted_iota(jnp.int32, (ROWS, 128), 1) < HEAD_DIM
    return jnp.where(left, even + pltpu.roll(even, HEAD_DIM, 1), odd + pltpu.roll(odd, HEAD_DIM, 1))


def columns_of(label_ref, core):
    blocks = [label_ref[:1, start:start + 32] for start in range(0, 512, 32)]
    sides = [jnp.concatenate(blocks[side::2], 1) for side in range(2)]
    return jnp.where(core == 0, sides[0], sides[1])


def grads_kernel(core_ref, q_ref, *refs):
    images = (refs[:5], refs[5:10])
    dq_ref, *image_refs = refs[10:13]
    e_ref, h_ref, o_ref, total_ref = refs[13:]
    width = HEADS * HEAD_DIM
    turned = q_ref[...].T
    columns = turned.shape[1]
    probe = lax.rsqrt(jnp.sum(turned * turned, axis=0, keepdims=True) / width + 1e-6)
    query_high, query_low = split(turned * (LOG2E / 8.0))
    below = lax.broadcasted_iota(jnp.int32, (16, columns), 0) < PATCHES - 192
    inverse, match, square = ([[], []] for _ in range(3))

    for head in range(HEADS):
        own = slice(head * HEAD_DIM, (head + 1) * HEAD_DIM)
        qh, ql = query_high[own], query_low[own]
        keys = jnp.concatenate([images[0][0][head], images[1][0][head]], 0)
        both = product(keys, jnp.concatenate([qh, ql, qh, ql], 0))
        for place in range(2):
            start = place * ROWS
            scores = jnp.concatenate([
                both[start:start + 192], jnp.where(below, both[start + 192:start + ROWS], -1e30)], 0)
            exponent = jnp.exp2(scores - jnp.max(scores, axis=0, keepdims=True))
            norm = 1.0 / jnp.sum(exponent, axis=0, keepdims=True)
            high, low = split(exponent)
            e_ref[head, start:start + ROWS, :] = exponent
            h_ref[head, 2 * start:2 * start + ROWS, :] = high
            h_ref[head, 2 * start + ROWS:2 * start + 2 * ROWS, :] = low
            vt_ref = images[place][3]
            wide = product(vt_ref[head], high)
            pooled = (wide[:HEAD_DIM] + wide[HEAD_DIM:] + product(vt_ref[head, :HEAD_DIM], low)) * norm
            o_ref[place, own, :] = pooled
            inverse[place].append(norm)
            match[place].append(jnp.sum(pooled * turned[own], axis=0, keepdims=True))
            square[place].append(jnp.sum(pooled * pooled, axis=0, keepdims=True))

    slopes = []
    for place in range(2):
        similar = sum(match[place]) / width
        summary = lax.rsqrt(sum(square[place]) / width + 1e-6)
        sign = 2.0 * columns_of(images[place][4], core_ref[0]) - 1.0
        logit = 10.0 * similar * summary * probe - 2.0
        slope = -sign / (1.0 + jnp.exp(sign * logit)) * (10.0 / width)
        alpha = slope * summary * probe
        slopes.append((alpha, -alpha * similar * summary * summary, -alpha * similar * probe * probe))
    gamma = slopes[0][2] + slopes[1][2]

    even = [None, None]
    for head in range(HEADS):
        own = slice(head * HEAD_DIM, (head + 1) * HEAD_DIM)
        query = turned[own]
        total = gamma * query
        parts = []
        value_parts = []
        for place in range(2):
            _, vc_ref, kt_ref, _, _ = images[place]
            start = place * ROWS
            alpha, beta, _ = slopes[place]
            norm = inverse[place][head]
            pooled = o_ref[place, own, :]
            gh, gl = split((alpha * norm) * query + (beta * norm) * pooled)
            delta = (alpha * match[place][head] + beta * square[place][head]) * norm
            inner = product(vc_ref[head], jnp.concatenate([gh, gl, gh, gl], 0))
            high, low = split(e_ref[head, start:start + ROWS, :] * (inner - delta))
            parts += [high, low]
            value = product(h_ref[head, 2 * start:2 * start + 2 * ROWS, :], jnp.concatenate([gh, gl], 0), True)
            value_parts.append(value[:ROWS] + value[ROWS:])
            wide = product(kt_ref[head], high)
            total += wide[:HEAD_DIM] + wide[HEAD_DIM:] + product(kt_ref[head, :HEAD_DIM], low) + alpha * pooled
        total_ref[own, :] = total
        keys = product(
            jnp.concatenate(parts, 0), jnp.concatenate([query_high[own], query_low[own]], 0), True)
        for place in range(2):
            start = 2 * place * ROWS
            key = keys[start:start + ROWS] + keys[start + ROWS:start + 2 * ROWS]
            if head % 2 == 0:
                even[place] = key, value_parts[place]
            else:
                lanes = slice((head - 1) * HEAD_DIM, (head + 1) * HEAD_DIM)
                image_refs[place][:ROWS, lanes] = folded(even[place][0], key) * LN2
                image_refs[place][PART:, lanes] = folded(even[place][1], value_parts[place])
    dq_ref[...] = total_ref[...].T


def in_vmem(*values):
    return [pltpu.with_memory_space_constraint(value, pltpu.VMEM) for value in values]


def grads(core, q, own, other):
    chunk = q.shape[0]
    total = pltpu.VMEM((2 * PART, 512), jnp.float32)
    return pl.pallas_call(
        grads_kernel,
        in_specs=[pl.BlockSpec(memory_space=pltpu.SMEM)] + [pl.BlockSpec(memory_space=pltpu.VMEM)] * 11,
        out_shape=(pltpu.VMEM((chunk, 512), jnp.float32), total, total),
        scratch_shapes=[
            pltpu.VMEM((HEADS, 2 * ROWS, chunk), jnp.float32),
            pltpu.VMEM((HEADS, 4 * ROWS, chunk), jnp.bfloat16),
            pltpu.VMEM((2, 512, chunk), jnp.float32),
            pltpu.VMEM((512, chunk), jnp.float32),
        ],
        name="grads",
        compiler_params=PARAMS,
    )(core, *in_vmem(q, *own, *other))


def finish_kernel(own_ref, received_ref, dk_ref, dv_ref):
    for start, out_ref in ((0, dk_ref), (PART, dv_ref)):
        rows = slice(start, start + PATCHES)
        out_ref[:, 0, :] = own_ref[rows, :] + received_ref[rows, :]


def finish(own, received):
    out = jax.ShapeDtypeStruct((PATCHES, 1, 512), jnp.float32)
    return pl.pallas_call(
        finish_kernel, out_shape=(out, out), name="finish", compiler_params=PARAMS,
    )(*in_vmem(own, received))


RING = ("y_hi", "x", "y_lo")


def spread(value, axis, count):
    return lax.all_to_all(jnp.broadcast_to(value[None], (count,) + value.shape), axis, 0, 0, tiled=True)


def swapped(value):
    return lax.ppermute(value, "core", [(0, 1), (1, 0)])


def per_device(patch_keys, patch_values, caption_queries, positive):
    core = lax.axis_index("core").astype(jnp.int32).reshape(1)
    packed = pack(patch_keys.swapaxes(0, 1), patch_values.swapaxes(0, 1), positive)
    row = spread(caption_queries, "z", 16).reshape(16, 512)
    row, packed = lax.optimization_barrier((row, packed))
    queries = spread(row, RING, 16).reshape(256, 512)
    other = swapped(packed)
    queries, packed, other = lax.optimization_barrier((queries, packed, other))
    dq, own, foreign = grads(core, queries, prepare(packed), prepare(other))
    total = lax.all_to_all(dq.reshape(16, 16, 512), RING, 0, 0, tiled=True).sum(0)
    received = swapped(foreign)
    total = lax.all_to_all(total.reshape(16, 1, 512), "z", 0, 0, tiled=True).sum(0)
    grad_keys, grad_values = finish(own, received)
    return grad_keys.swapaxes(0, 1), grad_values.swapaxes(0, 1), total


AXES = ("y_hi", "x", "core", "y_lo", "z")


def solution(mesh):
    fine = Mesh(mesh.devices.reshape(2, 4, 2, 2, 16), AXES)
    return jax.shard_map(
        per_device, mesh=fine,
        in_specs=(P(AXES, None, None), P(AXES, None, None), P(AXES, None), P(AXES, None)),
        out_specs=(P(AXES, None, None), P(AXES, None, None), P(AXES, None)),
        check_vma=False,
    )
```

```python
import math

import jax
import jax.numpy as jnp
from jax import lax
from jax.experimental import pallas as pl
from jax.experimental.pallas import tpu as pltpu
from jax.sharding import Mesh
from jax.sharding import PartitionSpec as P


HEADS = 8
HEAD_DIM = 64
PATCHES = 196
ROWS = 208
PART = 208
LOG2E = math.log2(math.e)
LN2 = math.log(2.0)
PARAMS = pltpu.CompilerParams(vmem_limit_bytes=24 * 1024 * 1024)


def split(x):
    high = x.astype(jnp.bfloat16)
    return high, (x - high.astype(jnp.float32)).astype(jnp.bfloat16)


def product(lhs, rhs, transposed=False):
    contract = ((1,), (1 if transposed else 0,))
    return lax.dot_general(lhs, rhs, (contract, ((), ())), preferred_element_type=jnp.float32)


def pack_kernel(k_ref, v_ref, label_ref, out_ref):
    out_ref[:PATCHES, :] = k_ref[:, 0, :]
    out_ref[PART:PART + PATCHES, :] = v_ref[:, 0, :]
    labels = jnp.broadcast_to(label_ref[...].astype(jnp.float32), (8, 512))
    out_ref[2 * PART - 8:, :] = labels


def pack(k, v, label):
    return pl.pallas_call(
        pack_kernel,
        out_shape=pltpu.VMEM((2 * PART, 512), jnp.float32),
        name="pack",
        compiler_params=PARAMS,
    )(k, v, label)


def prepare_image(packed_ref, kc_ref, vc_ref, kt_ref, vt_ref, pad_ref):
    left = lax.broadcasted_iota(jnp.int32, (ROWS, 128), 1) < HEAD_DIM
    for start, cat_ref, turned_ref, scale in ((0, kc_ref, kt_ref, 0.125), (PART, vc_ref, vt_ref, 1.0)):
        pad_ref[192:, :] = jnp.zeros((64, 512), jnp.float32)
        pad_ref[:PATCHES, :] = packed_ref[start:start + PATCHES, :]
        for pair in range(HEADS // 2):
            tile = pad_ref[:, pair * 128:(pair + 1) * 128]
            rows = tile[:ROWS]
            high = rows.astype(jnp.bfloat16).astype(jnp.float32)
            for place, part in ((0, high), (1, rows - high)):
                rolled = pltpu.roll(part, HEAD_DIM, 1)
                lanes = slice(place * 128, (place + 1) * 128)
                cat_ref[2 * pair, :, lanes] = jnp.where(left, part, rolled).astype(jnp.bfloat16)
                cat_ref[2 * pair + 1, :, lanes] = jnp.where(left, rolled, part).astype(jnp.bfloat16)
            turned_high, turned_low = split(tile.T * scale)
            for side in range(2):
                own = slice(side * HEAD_DIM, (side + 1) * HEAD_DIM)
                turned_ref[2 * pair + side, :HEAD_DIM, :] = turned_high[own, :ROWS]
                turned_ref[2 * pair + side, HEAD_DIM:, :] = turned_low[own, :ROWS]


def folded(even, odd):
    left = lax.broadcasted_iota(jnp.int32, (ROWS, 128), 1) < HEAD_DIM
    return jnp.where(left, even + pltpu.roll(even, HEAD_DIM, 1), odd + pltpu.roll(odd, HEAD_DIM, 1))


def columns_of(label_ref, core):
    blocks = [label_ref[:1, start:start + 32] for start in range(0, 512, 32)]
    sides = [jnp.concatenate(blocks[side::2], 1) for side in range(2)]
    return jnp.where(core == 0, sides[0], sides[1])


def grads_kernel(core_ref, q_ref, *refs):
    packed = refs[:2]
    dq_ref, own_ref, foreign_ref = refs[2:5]
    e_ref, h_ref, o_ref, tile_ref, sems, image_ref, image_sems = refs[5:12]
    image_refs = image_ref, foreign_ref
    images = []
    for place in range(2):
        arrays = refs[12 + 5 * place:17 + 5 * place]
        prepare_image(packed[place], *arrays)
        images.append((*arrays[:4], packed[place].at[2 * PART - 8:, :]))
    width = HEADS * HEAD_DIM
    turned = q_ref[...].T
    columns = turned.shape[1]
    probe = lax.rsqrt(jnp.sum(turned * turned, axis=0, keepdims=True) / width + 1e-6)
    query_high, query_low = split(turned * (LOG2E / 8.0))
    below = lax.broadcasted_iota(jnp.int32, (16, columns), 0) < PATCHES - 192
    inverse, match, square = ([[], []] for _ in range(3))

    for head in range(HEADS):
        own = slice(head * HEAD_DIM, (head + 1) * HEAD_DIM)
        qh, ql = query_high[own], query_low[own]
        keys = jnp.concatenate([images[0][0][head], images[1][0][head]], 0)
        both = product(keys, jnp.concatenate([qh, ql, qh, ql], 0))
        for place in range(2):
            start = place * ROWS
            scores = jnp.concatenate([
                both[start:start + 192], jnp.where(below, both[start + 192:start + ROWS], -1e30)], 0)
            exponent = jnp.exp2(scores - jnp.max(scores, axis=0, keepdims=True))
            norm = 1.0 / jnp.sum(exponent, axis=0, keepdims=True)
            high, low = split(exponent)
            e_ref[head, start:start + ROWS, :] = exponent
            h_ref[head, 2 * start:2 * start + ROWS, :] = high
            h_ref[head, 2 * start + ROWS:2 * start + 2 * ROWS, :] = low
            vt_ref = images[place][3]
            wide = product(vt_ref[head], high)
            pooled = (wide[:HEAD_DIM] + wide[HEAD_DIM:] + product(vt_ref[head, :HEAD_DIM], low)) * norm
            o_ref[place, own, :] = pooled
            inverse[place].append(norm)
            match[place].append(jnp.sum(pooled * turned[own], axis=0, keepdims=True))
            square[place].append(jnp.sum(pooled * pooled, axis=0, keepdims=True))

    slopes = []
    for place in range(2):
        similar = sum(match[place]) / width
        summary = lax.rsqrt(sum(square[place]) / width + 1e-6)
        sign = 2.0 * columns_of(images[place][4], core_ref[0]) - 1.0
        logit = 10.0 * similar * summary * probe - 2.0
        slope = -sign / (1.0 + jnp.exp(sign * logit)) * (10.0 / width)
        alpha = slope * summary * probe
        slopes.append((alpha, -alpha * similar * summary * summary, -alpha * similar * probe * probe))
    gamma = slopes[0][2] + slopes[1][2]

    even = [None, None]
    parts_of_pair = []
    copies = []
    for head in range(HEADS):
        own = slice(head * HEAD_DIM, (head + 1) * HEAD_DIM)
        query = turned[own]
        total = gamma * query
        parts = []
        value_parts = []
        for place in range(2):
            _, vc_ref, kt_ref, _, _ = images[place]
            start = place * ROWS
            alpha, beta, _ = slopes[place]
            norm = inverse[place][head]
            pooled = o_ref[place, own, :]
            gh, gl = split((alpha * norm) * query + (beta * norm) * pooled)
            delta = (alpha * match[place][head] + beta * square[place][head]) * norm
            inner = product(vc_ref[head], jnp.concatenate([gh, gl, gh, gl], 0))
            high, low = split(e_ref[head, start:start + ROWS, :] * (inner - delta))
            parts += [high, low]
            value = product(h_ref[head, 2 * start:2 * start + 2 * ROWS, :], jnp.concatenate([gh, gl], 0), True)
            value_parts.append(value[:ROWS] + value[ROWS:])
            wide = product(kt_ref[head], high)
            total += wide[:HEAD_DIM] + wide[HEAD_DIM:] + product(kt_ref[head, :HEAD_DIM], low) + alpha * pooled
        parts_of_pair.append(total)
        keys = product(
            jnp.concatenate(parts, 0), jnp.concatenate([query_high[own], query_low[own]], 0), True)
        if head % 2 == 1:
            pair = head // 2
            lanes = slice(pair * 128, (pair + 1) * 128)
            tile_ref[:, lanes] = jnp.concatenate(parts_of_pair, 0).T
            parts_of_pair = []
            copies.append(pltpu.make_async_copy(tile_ref.at[:, lanes], dq_ref.at[:, lanes], sems.at[pair]))
            copies[-1].start()
        for place in range(2):
            start = 2 * place * ROWS
            key = keys[start:start + ROWS] + keys[start + ROWS:start + 2 * ROWS]
            if head % 2 == 0:
                even[place] = key, value_parts[place]
            else:
                lanes = slice((head - 1) * HEAD_DIM, (head + 1) * HEAD_DIM)
                image_refs[place][:ROWS, lanes] = folded(even[place][0], key) * LN2
                image_refs[place][PART:, lanes] = folded(even[place][1], value_parts[place])
        if head % 2 == 1:
            copies.append(pltpu.make_async_copy(image_ref.at[:, lanes], own_ref.at[:, lanes], image_sems.at[pair]))
            copies[-1].start()
    for copy in copies:
        copy.wait()


def in_vmem(*values):
    return [pltpu.with_memory_space_constraint(value, pltpu.VMEM) for value in values]


def grads(core, q, own, other):
    chunk = q.shape[0]
    total = pltpu.VMEM((2 * PART, 512), jnp.float32)
    cat = pltpu.VMEM((HEADS, ROWS, 256), jnp.bfloat16)
    turned = pltpu.VMEM((HEADS, 128, ROWS), jnp.bfloat16)
    vmem = pl.BlockSpec(memory_space=pltpu.VMEM)
    hbm = pl.BlockSpec(memory_space=pltpu.HBM)
    return pl.pallas_call(
        grads_kernel,
        in_specs=[pl.BlockSpec(memory_space=pltpu.SMEM)] + [vmem] * 3,
        out_specs=(hbm, hbm, vmem),
        out_shape=(pltpu.HBM((chunk, 512), jnp.float32), pltpu.HBM((2 * PART, 512), jnp.float32), total),
        scratch_shapes=[
            pltpu.VMEM((HEADS, 2 * ROWS, chunk), jnp.float32),
            pltpu.VMEM((HEADS, 4 * ROWS, chunk), jnp.bfloat16),
            pltpu.VMEM((2, 512, chunk), jnp.float32),
            pltpu.VMEM((chunk, 512), jnp.float32),
            pltpu.SemaphoreType.DMA((HEADS // 2,)),
            pltpu.VMEM((2 * PART, 512), jnp.float32),
            pltpu.SemaphoreType.DMA((HEADS // 2,)),
        ] + [cat, cat, turned, turned, pltpu.VMEM((256, 512), jnp.float32)] * 2,
        name="grads",
        compiler_params=PARAMS,
    )(core, *in_vmem(q, own, other))


def finish_kernel(own_ref, received_ref, dk_ref, dv_ref):
    for start, out_ref in ((0, dk_ref), (PART, dv_ref)):
        rows = slice(start, start + PATCHES)
        out_ref[:, 0, :] = own_ref[rows, :] + received_ref[rows, :]


def finish(own, received):
    out = jax.ShapeDtypeStruct((PATCHES, 1, 512), jnp.float32)
    return pl.pallas_call(
        finish_kernel, out_shape=(out, out), name="finish", compiler_params=PARAMS,
    )(*in_vmem(own, received))


RING = ("y_hi", "x", "y_lo")


def spread(value, axis, count):
    return lax.all_to_all(jnp.broadcast_to(value[None], (count,) + value.shape), axis, 0, 0, tiled=True)


def swapped(value):
    return lax.ppermute(value, "core", [(0, 1), (1, 0)])


def per_device(patch_keys, patch_values, caption_queries, positive):
    core = lax.axis_index("core").astype(jnp.int32).reshape(1)
    packed = pack(patch_keys.swapaxes(0, 1), patch_values.swapaxes(0, 1), positive)
    row = spread(caption_queries, "z", 16).reshape(16, 512)
    row, packed = lax.optimization_barrier((row, packed))
    queries = spread(row, RING, 16).reshape(256, 512)
    other = swapped(packed)
    queries, packed, other = lax.optimization_barrier((queries, packed, other))
    dq, own, foreign = grads(core, queries, packed, other)
    total = lax.all_to_all(dq.reshape(16, 16, 512), RING, 0, 0, tiled=True).sum(0)
    received = swapped(foreign)
    total = lax.all_to_all(total.reshape(16, 1, 512), "z", 0, 0, tiled=True).sum(0)
    grad_keys, grad_values = finish(own, received)
    return grad_keys.swapaxes(0, 1), grad_values.swapaxes(0, 1), total


AXES = ("y_hi", "x", "core", "y_lo", "z")


def solution(mesh):
    fine = Mesh(mesh.devices.reshape(2, 4, 2, 2, 16), AXES)
    return jax.shard_map(
        per_device, mesh=fine,
        in_specs=(P(AXES, None, None), P(AXES, None, None), P(AXES, None), P(AXES, None)),
        out_specs=(P(AXES, None, None), P(AXES, None, None), P(AXES, None)),
        check_vma=False,
    )
```

```python
import math

import jax
import jax.numpy as jnp
from jax import lax
from jax.experimental import pallas as pl
from jax.experimental.pallas import tpu as pltpu
from jax.sharding import Mesh
from jax.sharding import PartitionSpec as P


HEADS = 8
HEAD_DIM = 64
PATCHES = 196
ROWS = 208
PART = 208
LOG2E = math.log2(math.e)
LN2 = math.log(2.0)
PARAMS = pltpu.CompilerParams(vmem_limit_bytes=24 * 1024 * 1024)


def split(x):
    high = x.astype(jnp.bfloat16)
    return high, (x - high.astype(jnp.float32)).astype(jnp.bfloat16)


def product(lhs, rhs, transposed=False):
    contract = ((1,), (1 if transposed else 0,))
    return lax.dot_general(lhs, rhs, (contract, ((), ())), preferred_element_type=jnp.float32)


def pack_kernel(k_ref, v_ref, label_ref, out_ref, rows_ref, row_ref, sems):
    copies = [
        pltpu.make_async_copy(k_ref, rows_ref.at[0], sems.at[0]),
        pltpu.make_async_copy(v_ref, rows_ref.at[1], sems.at[1]),
        pltpu.make_async_copy(label_ref, row_ref, sems.at[2]),
    ]
    for copy in copies:
        copy.start()
    for copy in copies:
        copy.wait()
    out_ref[:PATCHES, :] = rows_ref[0, :, 0, :]
    out_ref[PART:PART + PATCHES, :] = rows_ref[1, :, 0, :]
    out_ref[2 * PART - 8:, :] = jnp.broadcast_to(row_ref[...].astype(jnp.float32), (8, 512))


def pack(k, v, label):
    values = [pltpu.with_memory_space_constraint(value, pltpu.HBM) for value in (k, v, label)]
    return pl.pallas_call(
        pack_kernel,
        in_specs=[pl.BlockSpec(memory_space=pltpu.HBM)] * 3,
        out_specs=pl.BlockSpec(memory_space=pltpu.VMEM),
        out_shape=pltpu.VMEM((2 * PART, 512), jnp.float32),
        scratch_shapes=[
            pltpu.VMEM((2, PATCHES, 1, 512), jnp.float32),
            pltpu.VMEM((1, 512), jnp.int32),
            pltpu.SemaphoreType.DMA((3,)),
        ],
        name="pack",
        compiler_params=PARAMS,
    )(*values)


def prepare_image(packed_ref, kc_ref, vc_ref, kt_ref, vt_ref, pad_ref):
    left = lax.broadcasted_iota(jnp.int32, (ROWS, 128), 1) < HEAD_DIM
    for start, cat_ref, turned_ref, scale in ((0, kc_ref, kt_ref, 0.125), (PART, vc_ref, vt_ref, 1.0)):
        pad_ref[192:, :] = jnp.zeros((64, 512), jnp.float32)
        pad_ref[:PATCHES, :] = packed_ref[start:start + PATCHES, :]
        for pair in range(HEADS // 2):
            tile = pad_ref[:, pair * 128:(pair + 1) * 128]
            rows = tile[:ROWS]
            high = rows.astype(jnp.bfloat16).astype(jnp.float32)
            for place, part in ((0, high), (1, rows - high)):
                rolled = pltpu.roll(part, HEAD_DIM, 1)
                lanes = slice(place * 128, (place + 1) * 128)
                cat_ref[2 * pair, :, lanes] = jnp.where(left, part, rolled).astype(jnp.bfloat16)
                cat_ref[2 * pair + 1, :, lanes] = jnp.where(left, rolled, part).astype(jnp.bfloat16)
            turned_high, turned_low = split(tile.T * scale)
            for side in range(2):
                own = slice(side * HEAD_DIM, (side + 1) * HEAD_DIM)
                turned_ref[2 * pair + side, :HEAD_DIM, :] = turned_high[own, :ROWS]
                turned_ref[2 * pair + side, HEAD_DIM:, :] = turned_low[own, :ROWS]


def folded(even, odd):
    left = lax.broadcasted_iota(jnp.int32, (ROWS, 128), 1) < HEAD_DIM
    return jnp.where(left, even + pltpu.roll(even, HEAD_DIM, 1), odd + pltpu.roll(odd, HEAD_DIM, 1))


def columns_of(label_ref, core):
    blocks = [label_ref[:1, start:start + 32] for start in range(0, 512, 32)]
    sides = [jnp.concatenate(blocks[side::2], 1) for side in range(2)]
    return jnp.where(core == 0, sides[0], sides[1])


def grads_kernel(core_ref, q_ref, *refs):
    packed = refs[:2]
    dq_ref, own_ref, foreign_ref = refs[2:5]
    e_ref, h_ref, o_ref, tile_ref, sems, image_ref, image_sems = refs[5:12]
    image_refs = image_ref, foreign_ref
    images = []
    for place in range(2):
        arrays = refs[12 + 5 * place:17 + 5 * place]
        prepare_image(packed[place], *arrays)
        images.append((*arrays[:4], packed[place].at[2 * PART - 8:, :]))
    width = HEADS * HEAD_DIM
    turned = q_ref[...].T
    columns = turned.shape[1]
    probe = lax.rsqrt(jnp.sum(turned * turned, axis=0, keepdims=True) / width + 1e-6)
    query_high, query_low = split(turned * (LOG2E / 8.0))
    below = lax.broadcasted_iota(jnp.int32, (16, columns), 0) < PATCHES - 192
    inverse, match, square = ([[], []] for _ in range(3))

    for head in range(HEADS):
        own = slice(head * HEAD_DIM, (head + 1) * HEAD_DIM)
        qh, ql = query_high[own], query_low[own]
        keys = jnp.concatenate([images[0][0][head], images[1][0][head]], 0)
        both = product(keys, jnp.concatenate([qh, ql, qh, ql], 0))
        for place in range(2):
            start = place * ROWS
            scores = jnp.concatenate([
                both[start:start + 192], jnp.where(below, both[start + 192:start + ROWS], -1e30)], 0)
            exponent = jnp.exp2(scores - jnp.max(scores, axis=0, keepdims=True))
            norm = 1.0 / jnp.sum(exponent, axis=0, keepdims=True)
            high, low = split(exponent)
            e_ref[head, start:start + ROWS, :] = exponent
            h_ref[head, 2 * start:2 * start + ROWS, :] = high
            h_ref[head, 2 * start + ROWS:2 * start + 2 * ROWS, :] = low
            vt_ref = images[place][3]
            wide = product(vt_ref[head], high)
            pooled = (wide[:HEAD_DIM] + wide[HEAD_DIM:] + product(vt_ref[head, :HEAD_DIM], low)) * norm
            o_ref[place, own, :] = pooled
            inverse[place].append(norm)
            match[place].append(jnp.sum(pooled * turned[own], axis=0, keepdims=True))
            square[place].append(jnp.sum(pooled * pooled, axis=0, keepdims=True))

    slopes = []
    for place in range(2):
        similar = sum(match[place]) / width
        summary = lax.rsqrt(sum(square[place]) / width + 1e-6)
        sign = 2.0 * columns_of(images[place][4], core_ref[0]) - 1.0
        logit = 10.0 * similar * summary * probe - 2.0
        slope = -sign / (1.0 + jnp.exp(sign * logit)) * (10.0 / width)
        alpha = slope * summary * probe
        slopes.append((alpha, -alpha * similar * summary * summary, -alpha * similar * probe * probe))
    gamma = slopes[0][2] + slopes[1][2]

    even = [None, None]
    parts_of_pair = []
    copies = []
    for head in range(HEADS):
        own = slice(head * HEAD_DIM, (head + 1) * HEAD_DIM)
        query = turned[own]
        total = gamma * query
        parts = []
        value_parts = []
        for place in range(2):
            _, vc_ref, kt_ref, _, _ = images[place]
            start = place * ROWS
            alpha, beta, _ = slopes[place]
            norm = inverse[place][head]
            pooled = o_ref[place, own, :]
            gh, gl = split((alpha * norm) * query + (beta * norm) * pooled)
            delta = (alpha * match[place][head] + beta * square[place][head]) * norm
            inner = product(vc_ref[head], jnp.concatenate([gh, gl, gh, gl], 0))
            high, low = split(e_ref[head, start:start + ROWS, :] * (inner - delta))
            parts += [high, low]
            value = product(h_ref[head, 2 * start:2 * start + 2 * ROWS, :], jnp.concatenate([gh, gl], 0), True)
            value_parts.append(value[:ROWS] + value[ROWS:])
            wide = product(kt_ref[head], high)
            total += wide[:HEAD_DIM] + wide[HEAD_DIM:] + product(kt_ref[head, :HEAD_DIM], low) + alpha * pooled
        parts_of_pair.append(total)
        keys = product(
            jnp.concatenate(parts, 0), jnp.concatenate([query_high[own], query_low[own]], 0), True)
        if head % 2 == 1:
            pair = head // 2
            lanes = slice(pair * 128, (pair + 1) * 128)
            tile_ref[:, lanes] = jnp.concatenate(parts_of_pair, 0).T
            parts_of_pair = []
            copies.append(pltpu.make_async_copy(tile_ref.at[:, lanes], dq_ref.at[:, lanes], sems.at[pair]))
            copies[-1].start()
        for place in range(2):
            start = 2 * place * ROWS
            key = keys[start:start + ROWS] + keys[start + ROWS:start + 2 * ROWS]
            if head % 2 == 0:
                even[place] = key, value_parts[place]
            else:
                lanes = slice((head - 1) * HEAD_DIM, (head + 1) * HEAD_DIM)
                image_refs[place][:ROWS, lanes] = folded(even[place][0], key) * LN2
                image_refs[place][PART:, lanes] = folded(even[place][1], value_parts[place])
        if head % 2 == 1:
            copies.append(pltpu.make_async_copy(image_ref.at[:, lanes], own_ref.at[:, lanes], image_sems.at[pair]))
            copies[-1].start()
    for copy in copies:
        copy.wait()


def in_vmem(*values):
    return [pltpu.with_memory_space_constraint(value, pltpu.VMEM) for value in values]


def grads(core, q, own, other):
    chunk = q.shape[0]
    total = pltpu.VMEM((2 * PART, 512), jnp.float32)
    cat = pltpu.VMEM((HEADS, ROWS, 256), jnp.bfloat16)
    turned = pltpu.VMEM((HEADS, 128, ROWS), jnp.bfloat16)
    vmem = pl.BlockSpec(memory_space=pltpu.VMEM)
    hbm = pl.BlockSpec(memory_space=pltpu.HBM)
    return pl.pallas_call(
        grads_kernel,
        in_specs=[pl.BlockSpec(memory_space=pltpu.SMEM)] + [vmem] * 3,
        out_specs=(hbm, hbm, vmem),
        out_shape=(pltpu.HBM((chunk, 512), jnp.float32), pltpu.HBM((2 * PART, 512), jnp.float32), total),
        scratch_shapes=[
            pltpu.VMEM((HEADS, 2 * ROWS, chunk), jnp.float32),
            pltpu.VMEM((HEADS, 4 * ROWS, chunk), jnp.bfloat16),
            pltpu.VMEM((2, 512, chunk), jnp.float32),
            pltpu.VMEM((chunk, 512), jnp.float32),
            pltpu.SemaphoreType.DMA((HEADS // 2,)),
            pltpu.VMEM((2 * PART, 512), jnp.float32),
            pltpu.SemaphoreType.DMA((HEADS // 2,)),
        ] + [cat, cat, turned, turned, pltpu.VMEM((256, 512), jnp.float32)] * 2,
        name="grads",
        compiler_params=PARAMS,
    )(core, *in_vmem(q, own, other))


def finish_kernel(own_ref, received_ref, dk_ref, dv_ref):
    for start, out_ref in ((0, dk_ref), (PART, dv_ref)):
        rows = slice(start, start + PATCHES)
        out_ref[:, 0, :] = own_ref[rows, :] + received_ref[rows, :]


def finish(own, received):
    out = jax.ShapeDtypeStruct((PATCHES, 1, 512), jnp.float32)
    return pl.pallas_call(
        finish_kernel, out_shape=(out, out), name="finish", compiler_params=PARAMS,
    )(*in_vmem(own, received))


RING = ("y_hi", "x", "y_lo")


def spread(value, axis, count):
    return lax.all_to_all(jnp.broadcast_to(value[None], (count,) + value.shape), axis, 0, 0, tiled=True)


def swapped(value):
    return lax.ppermute(value, "core", [(0, 1), (1, 0)])


def per_device(patch_keys, patch_values, caption_queries, positive):
    core = lax.axis_index("core").astype(jnp.int32).reshape(1)
    packed = pack(patch_keys.swapaxes(0, 1), patch_values.swapaxes(0, 1), positive)
    row = spread(caption_queries, "z", 16).reshape(16, 512)
    row, packed = lax.optimization_barrier((row, packed))
    queries = spread(row, RING, 16).reshape(256, 512)
    other = swapped(packed)
    queries, packed, other = lax.optimization_barrier((queries, packed, other))
    dq, own, foreign = grads(core, queries, packed, other)
    total = lax.all_to_all(dq.reshape(16, 16, 512), RING, 0, 0, tiled=True).sum(0)
    received = swapped(foreign)
    total = lax.all_to_all(total.reshape(16, 1, 512), "z", 0, 0, tiled=True).sum(0)
    grad_keys, grad_values = finish(own, received)
    return grad_keys.swapaxes(0, 1), grad_values.swapaxes(0, 1), total


AXES = ("y_hi", "x", "core", "y_lo", "z")


def solution(mesh):
    fine = Mesh(mesh.devices.reshape(2, 4, 2, 2, 16), AXES)
    return jax.shard_map(
        per_device, mesh=fine,
        in_specs=(P(AXES, None, None), P(AXES, None, None), P(AXES, None), P(AXES, None)),
        out_specs=(P(AXES, None, None), P(AXES, None, None), P(AXES, None)),
        check_vma=False,
    )
```
